32 devices in a mesh: gx: 4 (over z), gy: 4 (over x, core), gz: 2 (over y).
Axes of the slice: x: 2, y: 2, z: 4, core: 2. Of those that a mesh axis runs over, the one named last changes fastest.
Arguments:
- order_real: float32 [32, 256, 512], P('gz', 'gx', 'gy'), may hold values from -2.5 to 2.5
- order_imag: float32 [32, 256, 512], P('gz', 'gx', 'gy'), may hold values from -2.5 to 2.5
- phase_z: float32 [32, 256, 512], P('gz', 'gx', 'gy'), may hold values from -3.140625 to 3.140625
- phase_x: float32 [32, 256, 512], P('gz', 'gx', 'gy'), may hold values from -3.140625 to 3.140625
- phase_y: float32 [32, 256, 512], P('gz', 'gx', 'gy'), may hold values from -3.140625 to 3.140625
- material: int32 [32, 256, 512], P('gz', 'gx', 'gy'), may hold values from 0 to 7
- levels: float32 [8], replicated, may hold values from -0.5 to 1.5
Outputs:
- final_real: float32 [32, 256, 512], P('gz', 'gx', 'gy')
- final_imag: float32 [32, 256, 512], P('gz', 'gx', 'gy')
- circulation: float32 [32, 256, 512], P('gz', ('gx', 'gy'))
- current_flux: float32 [32, 256, 512], P('gz', ('gx', 'gy'))
The draws below stay inside these ranges and needn't reach their ends.
All inputs are finite; a program needn't handle non-finite values.
Results may differ from the reference program's by a relative error of at most 0.0003.
Values sent between devices are 32-bit elements; how exact they have to be, the bound alone decides.
A program may use at most 64 MiB of HBM per device.

```python
import jax
import jax.numpy as jnp

STEPS = 2
LEVELS = 8
NZ = 32
NX = 256
NY = 512


def place_ends(array, rng, least, top_value):
    longest = array.shape.index(max(array.shape))
    spots = []
    for shift in (0, 1):
        where = [jax.random.randint(jax.random.fold_in(rng, axis), (), 0, length) for axis, length in enumerate(array.shape)]
        where[longest] = (where[longest] + shift) % array.shape[longest]
        spots.append(tuple(where))
    return array.at[spots[0]].set(least).at[spots[1]].set(top_value)


def block_levels(own_key, extent, pieces, smallest, high):
    def one(position, shards_of):
        steps = jax.random.uniform(jax.random.fold_in(jax.random.fold_in(own_key, 6), position), (shards_of,), jnp.float32, smallest / len(pieces), high / len(pieces))
        return jnp.repeat(jnp.exp(steps), extent[position] // shards_of).reshape((-1,) + (1,) * (len(extent) - position - 1))

    loudness = one(*pieces[0])
    for cut in pieces[1:]:
        loudness = loudness * one(*cut)
    return loudness


def gaussian(stream_key, dims, deviation, reach, split=(), dtype=jnp.bfloat16):
    values = deviation * jax.random.normal(stream_key, dims, jnp.float32)
    if split:
        values = values * block_levels(stream_key, dims, split, -0.22, 0.18)
    return jnp.clip(values, -reach, reach).astype(dtype)


def setup_inputs(seed: int = 0) -> dict:
    arg_keys = jax.random.split(jax.random.key(seed), 8)
    order_real = gaussian(arg_keys[0], (NZ, NX, NY), 0.6, 2.5, ((0, 2), (1, 4), (2, 4)), jnp.float32)
    order_imag = gaussian(arg_keys[1], (NZ, NX, NY), 0.6, 2.5, ((0, 2), (1, 4), (2, 4)), jnp.float32)
    phase_z = jnp.clip(jax.random.uniform(arg_keys[2], (NZ, NX, NY), jnp.float32, -3.140625, 3.140625), -3.140625, 3.140625)
    phase_x = jnp.clip(jax.random.uniform(arg_keys[3], (NZ, NX, NY), jnp.float32, -3.140625, 3.140625), -3.140625, 3.140625)
    phase_y = jnp.clip(jax.random.uniform(arg_keys[4], (NZ, NX, NY), jnp.float32, -3.140625, 3.140625), -3.140625, 3.140625)
    material = place_ends(jax.random.randint(arg_keys[5], (NZ, NX, NY), 0, LEVELS), jax.random.fold_in(arg_keys[5], 1), 0, LEVELS - 1).astype(jnp.int32)
    levels = jnp.clip(jax.random.uniform(arg_keys[6], (LEVELS,), jnp.float32, -0.5, 1.5), -0.5, 1.5)
    return dict(order_real=order_real, order_imag=order_imag, phase_z=phase_z, phase_x=phase_x, phase_y=phase_y, material=material, levels=levels)


time_step = 0.15


def inner(values, direction, offset):
    slicer = [slice(1, length - 1) for length in values.shape]
    length = values.shape[direction]
    slicer[direction] = slice(1 + offset, length - 1 + offset)
    return values[tuple(slicer)]


def advance(real_part, imag_part, cosines, sine_parts, epsilon, inside_mask):
    centre_real = inner(real_part, 0, 0)
    centre_imag = inner(imag_part, 0, 0)
    lap_real = -6.0 * centre_real
    lap_imag = -6.0 * centre_imag
    for direction in range(3):
        cosine = inner(cosines[direction], direction, 0)
        sine_part = inner(sine_parts[direction], direction, 0)
        ahead_real = inner(real_part, direction, 1)
        ahead_imag = inner(imag_part, direction, 1)
        lap_real = lap_real + cosine * ahead_real - sine_part * ahead_imag
        lap_imag = lap_imag + cosine * ahead_imag + sine_part * ahead_real
        cosine = inner(cosines[direction], direction, -1)
        sine_part = inner(sine_parts[direction], direction, -1)
        behind_real = inner(real_part, direction, -1)
        behind_imag = inner(imag_part, direction, -1)
        lap_real = lap_real + cosine * behind_real + sine_part * behind_imag
        lap_imag = lap_imag + cosine * behind_imag - sine_part * behind_real
    density = centre_real * centre_real + centre_imag * centre_imag
    new_real = centre_real + time_step * ((epsilon - density) * centre_real + lap_real)
    new_imag = centre_imag + time_step * ((epsilon - density) * centre_imag + lap_imag)
    if inside_mask is not None:
        new_real = new_real * inside_mask
        new_imag = new_imag * inside_mask
    return new_real, new_imag


def current(first_real, first_imag, second_real, second_imag, phase):
    cosine = jnp.cos(phase)
    sine_part = jnp.sin(phase)
    turned_real = cosine * second_real - sine_part * second_imag
    turned_imag = cosine * second_imag + sine_part * second_real
    return first_real * turned_imag - first_imag * turned_real


def analyse(upper_real, upper_imag, phase_along_x, phase_along_y):
    rows = phase_along_x.shape[1]
    cols = phase_along_y.shape[2]
    current_x = current(upper_real[:, :rows, :], upper_imag[:, :rows, :], upper_real[:, 1:, :], upper_imag[:, 1:, :], phase_along_x)
    current_y = current(upper_real[:, :, :cols], upper_imag[:, :, :cols], upper_real[:, :, 1:], upper_imag[:, :, 1:], phase_along_y)
    circulation = current_x[:, :, :cols] + current_y[:, 1:, :] - current_x[:, :, 1:] - current_y[:, :rows, :]
    return circulation, current_x[:, :, :cols]


def reference(order_real, order_imag, phase_z, phase_x, phase_y, material, levels):
    epsilon = levels[material]
    padded = [jnp.pad(phase, 1) for phase in (phase_z, phase_x, phase_y)]
    cosines = [jnp.cos(phase) for phase in padded]
    sine_parts = [jnp.sin(phase) for phase in padded]
    real_part, imag_part = order_real, order_imag
    for turn in range(STEPS):
        real_part, imag_part = advance(jnp.pad(real_part, 1), jnp.pad(imag_part, 1), cosines, sine_parts, epsilon, None)
    upper = ((0, 0), (0, 1), (0, 1))
    circulation, current_x = analyse(jnp.pad(real_part, upper), jnp.pad(imag_part, upper),
                                     jnp.pad(phase_x, ((0, 0), (0, 0), (0, 1))), jnp.pad(phase_y, ((0, 0), (0, 1), (0, 0))))
    current_flux = jnp.cumsum(current_x, axis=2)
    return real_part, imag_part, circulation, current_flux
```

```python
import functools
import math

import jax
import jax.numpy as jnp
from jax import lax
from jax.experimental import pallas as pl
from jax.experimental.pallas import tpu as pltpu
from jax.sharding import PartitionSpec as P

STEPS = 2
LEVELS = 8
DT = 0.15
W = 128
MESH = pl.DeviceIdType.MESH

S = [(-1.0) ** k / (math.factorial(2 * k + 1) * 2.0 ** (2 * k + 1)) for k in range(7)]
C = [(-1.0) ** k / (math.factorial(2 * k) * 2.0 ** (2 * k)) for k in range(7)]


def poly(t, coefs):
    acc = jnp.float32(coefs[-1]) * t + jnp.float32(coefs[-2])
    for c in coefs[-3::-1]:
        acc = acc * t + jnp.float32(c)
    return acc


def cos_sin(x):
    t = x * x
    s = x * poly(t, S)
    c = poly(t, C)
    u = s + s
    return 1.0 - u * s, u * c


def iota(shape, dim):
    return lax.broadcasted_iota(jnp.int32, shape, dim)


def pack_cols(layers, col, nx):
    lane = iota((nx, W), 1)
    acc = jnp.zeros((nx, W), jnp.float32)
    for z, layer in enumerate(layers):
        shift = (z - col) % W
        moved = layer() if shift == 0 else pltpu.roll(layer(), shift, 1)
        acc = jnp.where(lane == z, moved, acc)
    return acc


def kernel(dims, o_r, o_i, p_z, p_x, p_y, mat, lev, fr, fi, circ, flux,
           cs, eps, st, zu_s, zd_s, xu_s, xd_s, yu_s, yd_s,
           zu_r, zd_r, xu_r, xd_r, yu_r, yd_r, ecx, ecy, ecz,
           jj, rj, e_s, e_r, snd, rcv, jsnd, jrcv, esnd, ercv):
    NZ, NX, R, GX, GY, GZ = dims
    gx, gy, gz = (lax.axis_index(a) for a in ("gx", "gy", "gz"))
    lane = iota((NX, W), 1)
    row = iota((NX, W), 0)
    G = GY

    here = {"gx": gx, "gy": gy, "gz": gz}

    def at_device(**other):
        return tuple({**here, **other}[a] for a in ("gx", "gy", "gz"))

    barrier = pltpu.get_barrier_semaphore()

    def greet(cond, who):
        @pl.when(cond)
        def _():
            pl.semaphore_signal(barrier, inc=1, device_id=who, device_id_type=MESH)

    peers = []
    for k in range(1, G):
        peers.append((gx >= 0, at_device(gy=lax.rem(gy + k, G))))
    peers.append((gx > 0, at_device(gx=jnp.maximum(gx - 1, 0))))
    peers.append((gx < GX - 1, at_device(gx=jnp.minimum(gx + 1, GX - 1))))
    peers.append((gz > 0, at_device(gz=jnp.maximum(gz - 1, 0))))
    peers.append((gz < GZ - 1, at_device(gz=jnp.minimum(gz + 1, GZ - 1))))
    peers.append(((gx > 0) & (gy < G - 1), at_device(gx=jnp.maximum(gx - 1, 0), gy=G - 1)))
    for s in range(G - 1):
        peers.append(((gx < GX - 1) & (gy == G - 1), at_device(gx=jnp.minimum(gx + 1, GX - 1), gy=s)))
    for cond, who in peers:
        greet(cond, who)

    up = {
        "z": (gz < GZ - 1, at_device(gz=jnp.minimum(gz + 1, GZ - 1)), gz > 0),
        "x": (gx < GX - 1, at_device(gx=jnp.minimum(gx + 1, GX - 1)), gx > 0),
        "y": (gy < G - 1, at_device(gy=jnp.minimum(gy + 1, G - 1)), gy > 0),
    }
    down = {
        "z": (gz > 0, at_device(gz=jnp.maximum(gz - 1, 0)), gz < GZ - 1),
        "x": (gx > 0, at_device(gx=jnp.maximum(gx - 1, 0)), gx < GX - 1),
        "y": (gy > 0, at_device(gy=jnp.maximum(gy - 1, 0)), gy < G - 1),
    }

    def messages(t):
        out = []
        full = [(yu_s, yu_r, up["y"]), (yd_s, yd_r, down["y"]), (xu_s, xu_r, up["x"]),
                (xd_s, xd_r, down["x"]), (zu_s, zu_r, up["z"]), (zd_s, zd_r, down["z"])]
        for m, (src, dst, (scond, who, rcond)) in enumerate(full):
            if t == STEPS and m not in (1, 3):
                continue
            copy = pltpu.make_async_remote_copy(
                src_ref=src.at[t], dst_ref=dst.at[t], send_sem=snd.at[t * 6 + m],
                recv_sem=rcv.at[t * 6 + m], device_id=who, device_id_type=MESH)
            out.append((copy, scond, rcond, dst.at[t]))
        return out

    rounds = [messages(t) for t in range(STEPS + 1)]

    for msgs in rounds:
        for _, _, rcond, dst in msgs:
            @pl.when(jnp.logical_not(rcond))
            def _(dst=dst):
                dst[...] = jnp.zeros_like(dst)

    def launch(t):
        for copy, scond, _, _ in rounds[t]:
            pl.when(scond)(copy.start)

    def arrive(t):
        for copy, _, rcond, _ in rounds[t]:
            pl.when(rcond)(copy.wait_recv)

    def edges(t, sr, si):
        first_r = pack_cols([lambda z=z: sr[z] for z in range(NZ)], 0, NX)
        first_i = pack_cols([lambda z=z: si[z] for z in range(NZ)], 0, NX)
        yd_s[t] = jnp.where(lane < NZ, first_r, pltpu.roll(first_i, NZ, 1))
        xd_s[t, 0] = sr[:, 0, :]
        xd_s[t, 1] = si[:, 0, :]
        if t == STEPS:
            return
        last_r = pack_cols([lambda z=z: sr[z] for z in range(NZ)], W - 1, NX)
        last_i = pack_cols([lambda z=z: si[z] for z in range(NZ)], W - 1, NX)
        c, s = ecy[0], ecy[1]
        qr, qi = c * last_r + s * last_i, c * last_i - s * last_r
        yu_s[t] = jnp.where(lane < NZ, qr, pltpu.roll(qi, NZ, 1))
        lr, li = sr[:, NX - 1, :], si[:, NX - 1, :]
        c, s = ecx[0], ecx[1]
        xu_s[t, 0] = c * lr + s * li
        xu_s[t, 1] = c * li - s * lr
        zd_s[t, 0] = sr[0]
        zd_s[t, 1] = si[0]
        c, s = ecz[0], ecz[1]
        lr, li = sr[NZ - 1], si[NZ - 1]
        zu_s[t, 0] = c * lr + s * li
        zu_s[t, 1] = c * li - s * lr

    ecx[0], ecx[1] = cos_sin(p_x[:, NX - 1, :])
    ecy[0], ecy[1] = cos_sin(pack_cols([lambda z=z: p_y[z] for z in range(NZ)], W - 1, NX))
    ecz[0], ecz[1] = cos_sin(p_z[NZ - 1])
    edges(0, o_r, o_i)
    count = jnp.int32(0)
    for cond, _ in peers:
        count = count + jnp.where(cond, 1, 0)
    pl.semaphore_wait(barrier, count)
    launch(0)

    def prepare(z, _):
        for m, ref in enumerate((p_z, p_x, p_y)):
            c, s = cos_sin(ref[z])
            cs[2 * m, z] = c
            cs[2 * m + 1, z] = s
        m = mat[z]
        b0, b1, b2 = (m & 1) != 0, (m & 2) != 0, (m & 4) != 0
        quarter = [jnp.where(b0, lev[2 * j + 1], lev[2 * j]) for j in range(4)]
        half = [jnp.where(b1, quarter[2 * j + 1], quarter[2 * j]) for j in range(2)]
        eps[z] = jnp.where(b2, half[1], half[0])
        return 0

    lax.fori_loop(0, NZ, prepare, 0)

    def ahead_x(t, part, z, v):
        halo = xd_r[t, part, pl.ds(z, 1), :]
        return jnp.where(row == NX - 1, halo, pltpu.roll(v, NX - 1, 0))

    def ahead_y(t, part, z, v):
        halo = pltpu.roll(yd_r[t], W - 1 - part * NZ - z, 1)
        return jnp.where(lane == W - 1, halo, pltpu.roll(v, W - 1, 1))

    def step(t, sr, si, dr, di):
        def body(z, carry, az_r, az_i):
            bz_r, bz_i = carry
            r, i = sr[z], si[z]
            lap_r = -6.0 * r + bz_r
            lap_i = -6.0 * i + bz_i
            c, s = cs[0, z], cs[1, z]
            lap_r = lap_r + c * az_r - s * az_i
            lap_i = lap_i + c * az_i + s * az_r
            nz_r, nz_i = c * r + s * i, c * i - s * r
            c, s = cs[2, z], cs[3, z]
            a_r, a_i = ahead_x(t, 0, z, r), ahead_x(t, 1, z, i)
            lap_r = lap_r + c * a_r - s * a_i
            lap_i = lap_i + c * a_i + s * a_r
            q_r, q_i = c * r + s * i, c * i - s * r
            lap_r = lap_r + jnp.where(row == 0, xu_r[t, 0, pl.ds(z, 1), :], pltpu.roll(q_r, 1, 0))
            lap_i = lap_i + jnp.where(row == 0, xu_r[t, 1, pl.ds(z, 1), :], pltpu.roll(q_i, 1, 0))
            c, s = cs[4, z], cs[5, z]
            a_r, a_i = ahead_y(t, 0, z, r), ahead_y(t, 1, z, i)
            lap_r = lap_r + c * a_r - s * a_i
            lap_i = lap_i + c * a_i + s * a_r
            q_r, q_i = c * r + s * i, c * i - s * r
            h_r = pltpu.roll(yu_r[t], (W - z) % W, 1)
            h_i = pltpu.roll(yu_r[t], W - NZ - z, 1)
            lap_r = lap_r + jnp.where(lane == 0, h_r, pltpu.roll(q_r, 1, 1))
            lap_i = lap_i + jnp.where(lane == 0, h_i, pltpu.roll(q_i, 1, 1))
            g = eps[z] - (r * r + i * i)
            dr[z] = r + DT * (g * r + lap_r)
            di[z] = i + DT * (g * i + lap_i)
            return nz_r, nz_i

        carry = (zu_r[t, 0], zu_r[t, 1])
        carry = lax.fori_loop(0, NZ - 1, lambda z, c: body(z, c, sr[z + 1], si[z + 1]), carry)
        body(NZ - 1, carry, zd_r[t, 0], zd_r[t, 1])

    s_r, s_i = st.at[0], st.at[1]
    arrive(0)
    step(0, o_r, o_i, s_r, s_i)
    edges(1, s_r, s_i)
    launch(1)
    arrive(1)
    step(1, s_r, s_i, fr, fi)
    edges(2, fr, fi)
    launch(2)
    arrive(2)

    mine = pl.ds(pl.multiple_of(gy * R, R), R)

    def currents(z, _):
        r, i = fr[z], fi[z]
        c, s = cs[2, z], cs[3, z]
        a_r, a_i = ahead_x(2, 0, z, r), ahead_x(2, 1, z, i)
        jj[0, z] = r * (c * a_i + s * a_r) - i * (c * a_r - s * a_i)
        c, s = cs[4, z], cs[5, z]
        a_r, a_i = ahead_y(2, 0, z, r), ahead_y(2, 1, z, i)
        j_y = r * (c * a_i + s * a_r) - i * (c * a_r - s * a_i)
        jj[1, z] = j_y
        for d in range(G):
            at = (R * (d + 1)) % NX
            e_s[d, pl.ds(z, 1), :] = j_y[at:at + 1, :]
        return 0

    lax.fori_loop(0, NZ, currents, 0)

    def slab_copy(k):
        to = lax.rem(gy + k, G)
        rows = pl.ds(pl.multiple_of(to * R, R), R)
        return pltpu.make_async_remote_copy(
            src_ref=jj.at[:, :, rows, :], dst_ref=rj.at[k], send_sem=jsnd.at[k],
            recv_sem=jrcv.at[k], device_id=at_device(gy=to), device_id_type=MESH)

    def row_copy(k):
        to = lax.rem(gy + k, G)
        return pltpu.make_async_remote_copy(
            src_ref=e_s.at[to], dst_ref=e_r.at[k], send_sem=esnd.at[k],
            recv_sem=ercv.at[k], device_id=at_device(gy=to), device_id_type=MESH)

    def last_row_copy(k):
        return pltpu.make_async_remote_copy(
            src_ref=e_s.at[G - 1], dst_ref=e_r.at[k], send_sem=esnd.at[G],
            recv_sem=ercv.at[k], device_id=at_device(gx=jnp.maximum(gx - 1, 0), gy=G - 1),
            device_id_type=MESH)

    slabs = [slab_copy(k) for k in range(1, G)]
    for copy in slabs:
        copy.start()
    for k in range(1, G):
        pl.when(lax.rem(gy + k, G) != G - 1)(row_copy(k).start)
    pl.when(gx > 0)(last_row_copy(G - 1 - gy).start)

    rj[0] = jj[:, :, mine, :]

    @pl.when(gy < G - 1)
    def _():
        e_r[0] = e_s[gy]

    @pl.when((gy == G - 1) & (gx == GX - 1))
    def _():
        e_r[...] = jnp.zeros_like(e_r)

    for copy in slabs:
        copy.wait_recv()

    @pl.when(gy < G - 1)
    def _():
        for k in range(1, G):
            row_copy(k).wait_recv()

    @pl.when((gy == G - 1) & (gx < GX - 1))
    def _():
        for k in range(G):
            last_row_copy(k).wait_recv()

    ZC = 4
    rows_n = ZC * R
    lane_s = iota((rows_n, W), 1)
    row_s = iota((ZC, R, W), 1)

    def slab(b, _):
        zs = pl.ds(b * ZC, ZC)
        slot = [lax.rem(gy - s + G, G) for s in range(G)]
        jx = [rj[slot[s], 0, zs].reshape(rows_n, W) for s in range(G)]
        total = jnp.zeros((rows_n, 1), jnp.float32)
        for s in range(G):
            v = jx[s]
            d = 1
            while d < W:
                v = v + jnp.where(lane_s >= d, pltpu.roll(v, d, 1), 0.0)
                d *= 2
            v = v + total
            total = v[:, W - 1:W]
            flux[zs, :, s * W:(s + 1) * W] = v.reshape(ZC, R, W)
            j_y = rj[slot[s], 1, zs]
            extra = e_r[slot[s], zs, :].reshape(ZC, 1, W)
            j_y_next = jnp.where(row_s == R - 1, extra, pltpu.roll(j_y, R - 1, 1))
            after = jx[s + 1][:, 0:1] if s < G - 1 else jnp.zeros((rows_n, 1), jnp.float32)
            j_x_next = jnp.where(lane_s == W - 1, after, pltpu.roll(jx[s], W - 1, 1))
            circ[zs, :, s * W:(s + 1) * W] = (
                (jx[s] - j_x_next).reshape(ZC, R, W) + j_y_next - j_y)
        return 0

    lax.fori_loop(0, NZ // ZC, slab, 0)

    for msgs in rounds:
        for copy, scond, _, _ in msgs:
            pl.when(scond)(copy.wait_send)
    for copy in slabs:
        copy.wait_send()
    for k in range(1, G):
        pl.when(lax.rem(gy + k, G) != G - 1)(row_copy(k).wait_send)
    pl.when(gx > 0)(last_row_copy(0).wait_send)


def solution(mesh):
    GX, GY, GZ = (mesh.shape[a] for a in ("gx", "gy", "gz"))

    def shards(o_r, o_i, p_z, p_x, p_y, mat, lev):
        NZ, NX, NY = o_r.shape
        assert NY == W and 2 * NZ <= W and NX % (8 * GY) == 0 and NZ % 4 == 0
        R = NX // GY
        f32 = jnp.float32
        T = STEPS + 1
        vm = lambda *shape: pltpu.VMEM(shape, f32)
        vspec = pl.BlockSpec(memory_space=pltpu.VMEM)
        sspec = pl.BlockSpec(memory_space=pltpu.SMEM)
        dma = pltpu.SemaphoreType.DMA
        layers = lambda: [vm(T, 2, NX, W), vm(T, 2, NX, W), vm(T, 2, NZ, W), vm(T, 2, NZ, W),
                          vm(T, NX, W), vm(T, NX, W)]
        return pl.pallas_call(
            functools.partial(kernel, (NZ, NX, R, GX, GY, GZ)),
            out_shape=[jax.ShapeDtypeStruct((NZ, NX, W), f32)] * 2
            + [jax.ShapeDtypeStruct((NZ, R, GY * W), f32)] * 2,
            in_specs=[vspec] * 6 + [sspec],
            out_specs=[vspec] * 4,
            scratch_shapes=[vm(6, NZ, NX, W), vm(NZ, NX, W), vm(2, NZ, NX, W)]
            + layers() + layers()
            + [vm(2, NZ, W), vm(2, NX, W), vm(2, NX, W),
               vm(2, NZ, NX, W), vm(GY, 2, NZ, R, W), vm(GY, NZ, W), vm(GY, NZ, W),
               dma((6 * T,)), dma((6 * T,)), dma((GY,)), dma((GY,)), dma((GY + 1,)), dma((GY,))],
            compiler_params=pltpu.CompilerParams(
                collective_id=0, has_side_effects=True, vmem_limit_bytes=48 * 1024 * 1024),
        )(o_r, o_i, p_z, p_x, p_y, mat, lev)

    block = P("gz", "gx", "gy")
    line = P("gz", ("gx", "gy"), None)
    return jax.shard_map(shards, mesh=mesh, in_specs=(block,) * 6 + (P(),),
                         out_specs=(block, block, line, line), check_vma=False)
```

```python
import functools
import math

import jax
import jax.numpy as jnp
from jax import lax
from jax.experimental import pallas as pl
from jax.experimental.pallas import tpu as pltpu
from jax.sharding import PartitionSpec as P

STEPS = 2
LEVELS = 8
DT = 0.15
W = 128
ZC = 4
MESH = pl.DeviceIdType.MESH

S = [(-1.0) ** k / (math.factorial(2 * k + 1) * 2.0 ** (2 * k + 1)) for k in range(7)]
C = [(-1.0) ** k / (math.factorial(2 * k) * 2.0 ** (2 * k)) for k in range(7)]


def poly(t, coefs):
    acc = jnp.float32(coefs[-1]) * t + jnp.float32(coefs[-2])
    for c in coefs[-3::-1]:
        acc = acc * t + jnp.float32(c)
    return acc


def cos_sin(x):
    t = x * x
    s = x * poly(t, S)
    c = poly(t, C)
    u = s + s
    return 1.0 - u * s, u * c


def iota(shape, dim):
    return lax.broadcasted_iota(jnp.int32, shape, dim)


def pack_cols(layers, col, nx):
    lane = iota((nx, W), 1)
    acc = jnp.zeros((nx, W), jnp.float32)
    for z, layer in enumerate(layers):
        shift = (z - col) % W
        moved = layer() if shift == 0 else pltpu.roll(layer(), shift, 1)
        acc = jnp.where(lane == z, moved, acc)
    return acc


def kernel(dims, h0, h1, h2, h3, h4, h5, lev, fr, fi, circ, flux,
           o_r, o_i, p_z, p_x, p_y, mat, cs, eps, st, zu_s, zd_s, xu_s, xd_s, yu_s, yd_s,
           zu_r, zd_r, xu_r, xd_r, yu_r, yd_r, ecx, ecy, ecz,
           jj, rj, e_s, e_r, fx_s, fx_r, fy_s, fy_r,
           insem, snd, rcv, jsnd, jrcv, esnd, ercv, fsnd, frcv):
    NZ, NX, R, GX, GY, GZ = dims
    gx, gy, gz = (lax.axis_index(a) for a in ("gx", "gy", "gz"))
    lane = iota((NX, W), 1)
    row = iota((NX, W), 0)
    G = GY
    loads = [pltpu.make_async_copy(h, v, insem.at[n]) for n, (h, v) in enumerate(
        ((h3, p_x), (h4, p_y), (h0, o_r), (h1, o_i), (h2, p_z), (h5, mat)))]
    for load in loads:
        load.start()

    here = {"gx": gx, "gy": gy, "gz": gz}

    def at_device(**other):
        return tuple({**here, **other}[a] for a in ("gx", "gy", "gz"))

    barrier = pltpu.get_barrier_semaphore()

    def greet(cond, who):
        @pl.when(cond)
        def _():
            pl.semaphore_signal(barrier, inc=1, device_id=who, device_id_type=MESH)

    peers = []
    for k in range(1, G):
        peers.append((gx >= 0, at_device(gy=lax.rem(gy + k, G))))
    peers.append((gx > 0, at_device(gx=jnp.maximum(gx - 1, 0))))
    peers.append((gx < GX - 1, at_device(gx=jnp.minimum(gx + 1, GX - 1))))
    peers.append((gz > 0, at_device(gz=jnp.maximum(gz - 1, 0))))
    peers.append((gz < GZ - 1, at_device(gz=jnp.minimum(gz + 1, GZ - 1))))
    peers.append(((gx > 0) & (gy < G - 1), at_device(gx=jnp.maximum(gx - 1, 0), gy=G - 1)))
    for s in range(G - 1):
        peers.append(((gx < GX - 1) & (gy == G - 1), at_device(gx=jnp.minimum(gx + 1, GX - 1), gy=s)))
    for cond, who in peers:
        greet(cond, who)

    up = {
        "z": (gz < GZ - 1, at_device(gz=jnp.minimum(gz + 1, GZ - 1)), gz > 0),
        "x": (gx < GX - 1, at_device(gx=jnp.minimum(gx + 1, GX - 1)), gx > 0),
        "y": (gy < G - 1, at_device(gy=jnp.minimum(gy + 1, G - 1)), gy > 0),
    }
    down = {
        "z": (gz > 0, at_device(gz=jnp.maximum(gz - 1, 0)), gz < GZ - 1),
        "x": (gx > 0, at_device(gx=jnp.maximum(gx - 1, 0)), gx < GX - 1),
        "y": (gy > 0, at_device(gy=jnp.maximum(gy - 1, 0)), gy < G - 1),
    }

    def messages(t):
        out = []
        full = [(yu_s, yu_r, up["y"]), (yd_s, yd_r, down["y"]), (xu_s, xu_r, up["x"]),
                (xd_s, xd_r, down["x"]), (zu_s, zu_r, up["z"]), (zd_s, zd_r, down["z"])]
        for m, (src, dst, (scond, who, rcond)) in enumerate(full):
            copy = pltpu.make_async_remote_copy(
                src_ref=src.at[t], dst_ref=dst.at[t], send_sem=snd.at[t * 6 + m],
                recv_sem=rcv.at[t * 6 + m], device_id=who, device_id_type=MESH)
            out.append((copy, scond, rcond, dst.at[t]))
        return out

    rounds = [messages(t) for t in range(STEPS)]
    NB = NZ // ZC
    final = []
    for b in range(NB):
        pair = []
        for m, (src, dst, (scond, who, rcond)) in enumerate(
                ((fy_s, fy_r, down["y"]), (fx_s, fx_r, down["x"]))):
            copy = pltpu.make_async_remote_copy(
                src_ref=src.at[b], dst_ref=dst.at[b], send_sem=fsnd.at[2 * b + m],
                recv_sem=frcv.at[2 * b + m], device_id=who, device_id_type=MESH)
            pair.append((copy, scond, rcond, dst.at[b]))
        final.append(pair)

    for msgs in rounds + final:
        for _, _, rcond, dst in msgs:
            @pl.when(jnp.logical_not(rcond))
            def _(dst=dst):
                dst[...] = jnp.zeros_like(dst)

    def launch(msgs):
        for copy, scond, _, _ in msgs:
            pl.when(scond)(copy.start)

    def arrive(msgs):
        for copy, _, rcond, _ in msgs:
            pl.when(rcond)(copy.wait_recv)

    def edges(t, sr, si):
        first_r = pack_cols([lambda z=z: sr[z] for z in range(NZ)], 0, NX)
        first_i = pack_cols([lambda z=z: si[z] for z in range(NZ)], 0, NX)
        yd_s[t] = jnp.where(lane < NZ, first_r, pltpu.roll(first_i, NZ, 1))
        xd_s[t, 0] = sr[:, 0, :]
        xd_s[t, 1] = si[:, 0, :]
        last_r = pack_cols([lambda z=z: sr[z] for z in range(NZ)], W - 1, NX)
        last_i = pack_cols([lambda z=z: si[z] for z in range(NZ)], W - 1, NX)
        c, s = ecy[0], ecy[1]
        qr, qi = c * last_r + s * last_i, c * last_i - s * last_r
        yu_s[t] = jnp.where(lane < NZ, qr, pltpu.roll(qi, NZ, 1))
        lr, li = sr[:, NX - 1, :], si[:, NX - 1, :]
        c, s = ecx[0], ecx[1]
        xu_s[t, 0] = c * lr + s * li
        xu_s[t, 1] = c * li - s * lr
        zd_s[t, 0] = sr[0]
        zd_s[t, 1] = si[0]
        c, s = ecz[0], ecz[1]
        lr, li = sr[NZ - 1], si[NZ - 1]
        zu_s[t, 0] = c * lr + s * li
        zu_s[t, 1] = c * li - s * lr

    for load in loads[:5]:
        load.wait()
    ecx[0], ecx[1] = cos_sin(p_x[:, NX - 1, :])
    ecy[0], ecy[1] = cos_sin(pack_cols([lambda z=z: p_y[z] for z in range(NZ)], W - 1, NX))
    ecz[0], ecz[1] = cos_sin(p_z[NZ - 1])
    edges(0, o_r, o_i)
    count = jnp.int32(0)
    for cond, _ in peers:
        count = count + jnp.where(cond, 1, 0)
    pl.semaphore_wait(barrier, count)
    launch(rounds[0])
    loads[5].wait()

    def prepare(z, _):
        for m, ref in enumerate((p_z, p_x, p_y)):
            c, s = cos_sin(ref[z])
            cs[2 * m, z] = c
            cs[2 * m + 1, z] = s
        m = mat[z]
        b0, b1, b2 = (m & 1) != 0, (m & 2) != 0, (m & 4) != 0
        quarter = [jnp.where(b0, lev[2 * j + 1], lev[2 * j]) for j in range(4)]
        half = [jnp.where(b1, quarter[2 * j + 1], quarter[2 * j]) for j in range(2)]
        eps[z] = jnp.where(b2, half[1], half[0])
        return 0

    lax.fori_loop(0, NZ, prepare, 0)

    def ahead_x(t, part, z, v):
        halo = xd_r[t, part, pl.ds(z, 1), :]
        return jnp.where(row == NX - 1, halo, pltpu.roll(v, NX - 1, 0))

    def ahead_y(t, part, z, v):
        halo = pltpu.roll(yd_r[t], W - 1 - part * NZ - z, 1)
        return jnp.where(lane == W - 1, halo, pltpu.roll(v, W - 1, 1))

    def step(t, sr, si, dr, di):
        def body(z, carry, az_r, az_i):
            bz_r, bz_i = carry
            r, i = sr[z], si[z]
            lap_r = -6.0 * r + bz_r
            lap_i = -6.0 * i + bz_i
            c, s = cs[0, z], cs[1, z]
            lap_r = lap_r + c * az_r - s * az_i
            lap_i = lap_i + c * az_i + s * az_r
            nz_r, nz_i = c * r + s * i, c * i - s * r
            c, s = cs[2, z], cs[3, z]
            a_r, a_i = ahead_x(t, 0, z, r), ahead_x(t, 1, z, i)
            lap_r = lap_r + c * a_r - s * a_i
            lap_i = lap_i + c * a_i + s * a_r
            q_r, q_i = c * r + s * i, c * i - s * r
            lap_r = lap_r + jnp.where(row == 0, xu_r[t, 0, pl.ds(z, 1), :], pltpu.roll(q_r, 1, 0))
            lap_i = lap_i + jnp.where(row == 0, xu_r[t, 1, pl.ds(z, 1), :], pltpu.roll(q_i, 1, 0))
            c, s = cs[4, z], cs[5, z]
            a_r, a_i = ahead_y(t, 0, z, r), ahead_y(t, 1, z, i)
            lap_r = lap_r + c * a_r - s * a_i
            lap_i = lap_i + c * a_i + s * a_r
            q_r, q_i = c * r + s * i, c * i - s * r
            h_r = pltpu.roll(yu_r[t], (W - z) % W, 1)
            h_i = pltpu.roll(yu_r[t], W - NZ - z, 1)
            lap_r = lap_r + jnp.where(lane == 0, h_r, pltpu.roll(q_r, 1, 1))
            lap_i = lap_i + jnp.where(lane == 0, h_i, pltpu.roll(q_i, 1, 1))
            g = eps[z] - (r * r + i * i)
            dr[z] = r + DT * (g * r + lap_r)
            di[z] = i + DT * (g * i + lap_i)
            return nz_r, nz_i

        def run(start, stop, carry):
            inner = min(stop, NZ - 1)
            carry = lax.fori_loop(
                start, inner, lambda z, c: body(z, c, sr[z + 1], si[z + 1]), carry)
            if stop == NZ:
                carry = body(NZ - 1, carry, zd_r[t, 0], zd_r[t, 1])
            return carry

        return run

    s_r, s_i = st.at[0], st.at[1]
    arrive(rounds[0])
    step(0, o_r, o_i, s_r, s_i)(0, NZ, (zu_r[0, 0], zu_r[0, 1]))
    edges(1, s_r, s_i)
    launch(rounds[1])
    mine = pl.ds(pl.multiple_of(gy * R, R), R)

    def slab_copy(b, k):
        to = lax.rem(gy + k, G)
        rows = pl.ds(pl.multiple_of(to * R, R), R)
        return pltpu.make_async_remote_copy(
            src_ref=jj.at[b, :, :, rows, :], dst_ref=rj.at[b, k], send_sem=jsnd.at[b * G + k],
            recv_sem=jrcv.at[b * G + k], device_id=at_device(gy=to), device_id_type=MESH)

    def row_copy(b, k):
        to = lax.rem(gy + k, G)
        return pltpu.make_async_remote_copy(
            src_ref=e_s.at[b, to], dst_ref=e_r.at[b, k], send_sem=esnd.at[b * (G + 1) + k],
            recv_sem=ercv.at[b * G + k], device_id=at_device(gy=to), device_id_type=MESH)

    def last_row_copy(b, k):
        return pltpu.make_async_remote_copy(
            src_ref=e_s.at[b, G - 1], dst_ref=e_r.at[b, k], send_sem=esnd.at[b * (G + 1) + G],
            recv_sem=ercv.at[b * G + k],
            device_id=at_device(gx=jnp.maximum(gx - 1, 0), gy=G - 1), device_id_type=MESH)

    @pl.when((gy == G - 1) & (gx == GX - 1))
    def _():
        e_r[...] = jnp.zeros_like(e_r)

    def faces(b):
        zs = range(b * ZC, (b + 1) * ZC)
        first_r = pack_cols([lambda z=z: fr[z] for z in zs], 0, NX)
        first_i = pack_cols([lambda z=z: fi[z] for z in zs], 0, NX)
        fy_s[b] = jnp.where(lane < ZC, first_r, pltpu.roll(first_i, ZC, 1))
        for j, z in enumerate(zs):
            fx_s[b, j:j + 1, :] = fr[z, 0:1, :]
            fx_s[b, ZC + j:ZC + j + 1, :] = fi[z, 0:1, :]

    def currents(b):
        def near_x(part, j, v):
            halo = fx_r[b, pl.ds(part * ZC + j, 1), :]
            return jnp.where(row == NX - 1, halo, pltpu.roll(v, NX - 1, 0))

        def near_y(part, j, v):
            halo = pltpu.roll(fy_r[b], W - 1 - part * ZC - j, 1)
            return jnp.where(lane == W - 1, halo, pltpu.roll(v, W - 1, 1))

        def body(j, _):
            z = b * ZC + j
            r, i = fr[z], fi[z]
            c, s = cs[2, z], cs[3, z]
            a_r, a_i = near_x(0, j, r), near_x(1, j, i)
            jj[b, 0, j] = r * (c * a_i + s * a_r) - i * (c * a_r - s * a_i)
            c, s = cs[4, z], cs[5, z]
            a_r, a_i = near_y(0, j, r), near_y(1, j, i)
            j_y = r * (c * a_i + s * a_r) - i * (c * a_r - s * a_i)
            jj[b, 1, j] = j_y
            for d in range(G):
                at = (R * (d + 1)) % NX
                e_s[b, d, pl.ds(j, 1), :] = j_y[at:at + 1, :]
            return 0

        lax.fori_loop(0, ZC, body, 0)

    def send(b):
        for k in range(1, G):
            pl.when(lax.rem(gy + k, G) != G - 1)(row_copy(b, k).start)
        pl.when(gx > 0)(last_row_copy(b, G - 1 - gy).start)
        for k in range(1, G):
            slab_copy(b, k).start()
        rj[b, 0] = jj[b, :, :, mine, :]

        @pl.when(gy < G - 1)
        def _():
            e_r[b, 0] = e_s[b, gy]

    def receive(b):
        for k in range(1, G):
            slab_copy(b, k).wait_recv()

        @pl.when(gy < G - 1)
        def _():
            for k in range(1, G):
                row_copy(b, k).wait_recv()

        @pl.when((gy == G - 1) & (gx < GX - 1))
        def _():
            for k in range(G):
                last_row_copy(b, k).wait_recv()

    rows_n = ZC * R
    lane_s = iota((rows_n, W), 1)
    row_s = iota((ZC, R, W), 1)
    slot = [lax.rem(gy - s + G, G) for s in range(G)]

    def slab(b):
        zs = slice(b * ZC, (b + 1) * ZC)
        jx = [rj[b, slot[s], 0].reshape(rows_n, W) for s in range(G)]
        total = jnp.zeros((rows_n, 1), jnp.float32)
        for s in range(G):
            v = jx[s]
            d = 1
            while d < W:
                v = v + jnp.where(lane_s >= d, pltpu.roll(v, d, 1), 0.0)
                d *= 2
            v = v + total
            total = v[:, W - 1:W]
            flux[zs, :, s * W:(s + 1) * W] = v.reshape(ZC, R, W)
            j_y = rj[b, slot[s], 1]
            extra = e_r[b, slot[s]].reshape(ZC, 1, W)
            j_y_next = jnp.where(row_s == R - 1, extra, pltpu.roll(j_y, R - 1, 1))
            after = jx[s + 1][:, 0:1] if s < G - 1 else jnp.zeros((rows_n, 1), jnp.float32)
            j_x_next = jnp.where(lane_s == W - 1, after, pltpu.roll(jx[s], W - 1, 1))
            circ[zs, :, s * W:(s + 1) * W] = (
                (jx[s] - j_x_next).reshape(ZC, R, W) + j_y_next - j_y)

    arrive(rounds[1])
    second = step(1, s_r, s_i, fr, fi)
    carry = (zu_r[1, 0], zu_r[1, 1])
    for b in range(NB + 1):
        if b < NB:
            carry = second(b * ZC, (b + 1) * ZC, carry)
            faces(b)
            launch(final[b])
        if b > 0:
            arrive(final[b - 1])
            currents(b - 1)
            send(b - 1)
    for b in range(NB):
        receive(b)
        slab(b)

    for msgs in rounds + final:
        for copy, scond, _, _ in msgs:
            pl.when(scond)(copy.wait_send)
    for b in range(NB):
        for k in range(1, G):
            slab_copy(b, k).wait_send()
            pl.when(lax.rem(gy + k, G) != G - 1)(row_copy(b, k).wait_send)
        pl.when(gx > 0)(last_row_copy(b, 0).wait_send)


def solution(mesh):
    GX, GY, GZ = (mesh.shape[a] for a in ("gx", "gy", "gz"))

    def shards(o_r, o_i, p_z, p_x, p_y, mat, lev):
        NZ, NX, NY = o_r.shape
        assert NY == W and 2 * NZ <= W and NX % (8 * GY) == 0 and NZ % ZC == 0
        R = NX // GY
        f32 = jnp.float32
        T = STEPS
        NB = NZ // ZC
        vm = lambda *shape: pltpu.VMEM(shape, f32)
        vspec = pl.BlockSpec(memory_space=pltpu.VMEM)
        hspec = pl.BlockSpec(memory_space=pl.ANY)
        sspec = pl.BlockSpec(memory_space=pltpu.SMEM)
        dma = pltpu.SemaphoreType.DMA
        layers = lambda: [vm(T, 2, NX, W), vm(T, 2, NX, W), vm(T, 2, NZ, W), vm(T, 2, NZ, W),
                          vm(T, NX, W), vm(T, NX, W)]
        return pl.pallas_call(
            functools.partial(kernel, (NZ, NX, R, GX, GY, GZ)),
            out_shape=[jax.ShapeDtypeStruct((NZ, NX, W), f32)] * 2
            + [jax.ShapeDtypeStruct((NZ, R, GY * W), f32)] * 2,
            in_specs=[hspec] * 6 + [sspec],
            out_specs=[vspec] * 4,
            scratch_shapes=[vm(NZ, NX, W)] * 5 + [pltpu.VMEM((NZ, NX, W), jnp.int32)]
            + [vm(6, NZ, NX, W), vm(NZ, NX, W), vm(2, NZ, NX, W)]
            + layers() + layers()
            + [vm(2, NZ, W), vm(2, NX, W), vm(2, NX, W),
               vm(NB, 2, ZC, NX, W), vm(NB, GY, 2, ZC, R, W), vm(NB, GY, ZC, W), vm(NB, GY, ZC, W),
               vm(NB, 2 * ZC, W), vm(NB, 2 * ZC, W), vm(NB, NX, W), vm(NB, NX, W),
               dma((6,)), dma((6 * T,)), dma((6 * T,)), dma((NB * GY,)), dma((NB * GY,)),
               dma((NB * (GY + 1),)), dma((NB * GY,)), dma((2 * NB,)), dma((2 * NB,))],
            compiler_params=pltpu.CompilerParams(
                collective_id=0, has_side_effects=True, vmem_limit_bytes=60 * 1024 * 1024),
        )(o_r, o_i, p_z, p_x, p_y, mat, lev)

    block = P("gz", "gx", "gy")
    line = P("gz", ("gx", "gy"), None)
    return jax.shard_map(shards, mesh=mesh, in_specs=(block,) * 6 + (P(),),
                         out_specs=(block, block, line, line), check_vma=False)
```

```python
import functools
import math

import jax
import jax.numpy as jnp
from jax import lax
from jax.experimental import pallas as pl
from jax.experimental.pallas import tpu as pltpu
from jax.sharding import PartitionSpec as P

STEPS = 2
LEVELS = 8
DT = 0.15
W = 128
ZC = 4
MESH = pl.DeviceIdType.MESH

S = [(-1.0) ** k / (math.factorial(2 * k + 1) * 2.0 ** (2 * k + 1)) for k in range(7)]
C = [(-1.0) ** k / (math.factorial(2 * k) * 2.0 ** (2 * k)) for k in range(7)]


def poly(t, coefs):
    acc = jnp.float32(coefs[-1]) * t + jnp.float32(coefs[-2])
    for c in coefs[-3::-1]:
        acc = acc * t + jnp.float32(c)
    return acc


def cos_sin(x):
    t = x * x
    s = x * poly(t, S)
    c = poly(t, C)
    u = s + s
    return 1.0 - u * s, u * c


def iota(shape, dim):
    return lax.broadcasted_iota(jnp.int32, shape, dim)


def pack_cols(layers, col, nx):
    lane = iota((nx, W), 1)
    acc = jnp.zeros((nx, W), jnp.float32)
    for z, layer in enumerate(layers):
        shift = (z - col) % W
        moved = layer() if shift == 0 else pltpu.roll(layer(), shift, 1)
        acc = jnp.where(lane == z, moved, acc)
    return acc


def kernel(dims, h0, h1, h2, h3, h4, h5, lev, g0, g1, g2, g3,
           fr, fi, circ, flux, o_r, o_i, p_z, p_x, p_y, mat, cs, eps, st, zu_s, zd_s, xu_s, xd_s, yu_s, yd_s,
           zu_r, zd_r, xu_r, xd_r, yu_r, yd_r, ecx, ecy, ecz,
           jj, rj, e_s, e_r, fx_s, fx_r, fy_s, fy_r,
           insem, outsem, snd, rcv, jsnd, jrcv, esnd, ercv, fsnd, frcv):
    NZ, NX, R, GX, GY, GZ = dims
    gx, gy, gz = (lax.axis_index(a) for a in ("gx", "gy", "gz"))
    lane = iota((NX, W), 1)
    row = iota((NX, W), 0)
    G = GY
    loads = [pltpu.make_async_copy(h, v, insem.at[n]) for n, (h, v) in enumerate(
        ((h3, p_x), (h4, p_y), (h0, o_r), (h1, o_i), (h2, p_z), (h5, mat)))]
    for load in loads:
        load.start()

    here = {"gx": gx, "gy": gy, "gz": gz}

    def at_device(**other):
        return tuple({**here, **other}[a] for a in ("gx", "gy", "gz"))

    barrier = pltpu.get_barrier_semaphore()

    def greet(cond, who):
        @pl.when(cond)
        def _():
            pl.semaphore_signal(barrier, inc=1, device_id=who, device_id_type=MESH)

    peers = []
    for k in range(1, G):
        peers.append((gx >= 0, at_device(gy=lax.rem(gy + k, G))))
    peers.append((gx > 0, at_device(gx=jnp.maximum(gx - 1, 0))))
    peers.append((gx < GX - 1, at_device(gx=jnp.minimum(gx + 1, GX - 1))))
    peers.append((gz > 0, at_device(gz=jnp.maximum(gz - 1, 0))))
    peers.append((gz < GZ - 1, at_device(gz=jnp.minimum(gz + 1, GZ - 1))))
    peers.append(((gx > 0) & (gy < G - 1), at_device(gx=jnp.maximum(gx - 1, 0), gy=G - 1)))
    for s in range(G - 1):
        peers.append(((gx < GX - 1) & (gy == G - 1), at_device(gx=jnp.minimum(gx + 1, GX - 1), gy=s)))
    for cond, who in peers:
        greet(cond, who)

    up = {
        "z": (gz < GZ - 1, at_device(gz=jnp.minimum(gz + 1, GZ - 1)), gz > 0),
        "x": (gx < GX - 1, at_device(gx=jnp.minimum(gx + 1, GX - 1)), gx > 0),
        "y": (gy < G - 1, at_device(gy=jnp.minimum(gy + 1, G - 1)), gy > 0),
    }
    down = {
        "z": (gz > 0, at_device(gz=jnp.maximum(gz - 1, 0)), gz < GZ - 1),
        "x": (gx > 0, at_device(gx=jnp.maximum(gx - 1, 0)), gx < GX - 1),
        "y": (gy > 0, at_device(gy=jnp.maximum(gy - 1, 0)), gy < G - 1),
    }

    def messages(t):
        out = []
        full = [(yu_s, yu_r, up["y"]), (yd_s, yd_r, down["y"]), (xu_s, xu_r, up["x"]),
                (xd_s, xd_r, down["x"]), (zu_s, zu_r, up["z"]), (zd_s, zd_r, down["z"])]
        for m, (src, dst, (scond, who, rcond)) in enumerate(full):
            copy = pltpu.make_async_remote_copy(
                src_ref=src.at[t], dst_ref=dst.at[t], send_sem=snd.at[t * 6 + m],
                recv_sem=rcv.at[t * 6 + m], device_id=who, device_id_type=MESH)
            out.append((copy, scond, rcond, dst.at[t]))
        return out

    rounds = [messages(t) for t in range(STEPS)]
    NB = NZ // ZC
    final = []
    for b in range(NB):
        pair = []
        for m, (src, dst, (scond, who, rcond)) in enumerate(
                ((fy_s, fy_r, down["y"]), (fx_s, fx_r, down["x"]))):
            copy = pltpu.make_async_remote_copy(
                src_ref=src.at[b], dst_ref=dst.at[b], send_sem=fsnd.at[2 * b + m],
                recv_sem=frcv.at[2 * b + m], device_id=who, device_id_type=MESH)
            pair.append((copy, scond, rcond, dst.at[b]))
        final.append(pair)

    for msgs in rounds + final:
        for _, _, rcond, dst in msgs:
            @pl.when(jnp.logical_not(rcond))
            def _(dst=dst):
                dst[...] = jnp.zeros_like(dst)

    def launch(msgs):
        for copy, scond, _, _ in msgs:
            pl.when(scond)(copy.start)

    def arrive(msgs):
        for copy, _, rcond, _ in msgs:
            pl.when(rcond)(copy.wait_recv)

    def edges(t, sr, si):
        first_r = pack_cols([lambda z=z: sr[z] for z in range(NZ)], 0, NX)
        first_i = pack_cols([lambda z=z: si[z] for z in range(NZ)], 0, NX)
        yd_s[t] = jnp.where(lane < NZ, first_r, pltpu.roll(first_i, NZ, 1))
        xd_s[t, 0] = sr[:, 0, :]
        xd_s[t, 1] = si[:, 0, :]
        last_r = pack_cols([lambda z=z: sr[z] for z in range(NZ)], W - 1, NX)
        last_i = pack_cols([lambda z=z: si[z] for z in range(NZ)], W - 1, NX)
        c, s = ecy[0], ecy[1]
        qr, qi = c * last_r + s * last_i, c * last_i - s * last_r
        yu_s[t] = jnp.where(lane < NZ, qr, pltpu.roll(qi, NZ, 1))
        lr, li = sr[:, NX - 1, :], si[:, NX - 1, :]
        c, s = ecx[0], ecx[1]
        xu_s[t, 0] = c * lr + s * li
        xu_s[t, 1] = c * li - s * lr
        zd_s[t, 0] = sr[0]
        zd_s[t, 1] = si[0]
        c, s = ecz[0], ecz[1]
        lr, li = sr[NZ - 1], si[NZ - 1]
        zu_s[t, 0] = c * lr + s * li
        zu_s[t, 1] = c * li - s * lr

    for load in loads[:5]:
        load.wait()
    ecx[0], ecx[1] = cos_sin(p_x[:, NX - 1, :])
    ecy[0], ecy[1] = cos_sin(pack_cols([lambda z=z: p_y[z] for z in range(NZ)], W - 1, NX))
    ecz[0], ecz[1] = cos_sin(p_z[NZ - 1])
    edges(0, o_r, o_i)
    count = jnp.int32(0)
    for cond, _ in peers:
        count = count + jnp.where(cond, 1, 0)
    pl.semaphore_wait(barrier, count)
    launch(rounds[0])
    loads[5].wait()

    def prepare(z, _):
        for m, ref in enumerate((p_z, p_x, p_y)):
            c, s = cos_sin(ref[z])
            cs[2 * m, z] = c
            cs[2 * m + 1, z] = s
        m = mat[z]
        b0, b1, b2 = (m & 1) != 0, (m & 2) != 0, (m & 4) != 0
        quarter = [jnp.where(b0, lev[2 * j + 1], lev[2 * j]) for j in range(4)]
        half = [jnp.where(b1, quarter[2 * j + 1], quarter[2 * j]) for j in range(2)]
        eps[z] = jnp.where(b2, half[1], half[0])
        return 0

    lax.fori_loop(0, NZ, prepare, 0)

    def ahead_x(t, part, z, v):
        halo = xd_r[t, part, pl.ds(z, 1), :]
        return jnp.where(row == NX - 1, halo, pltpu.roll(v, NX - 1, 0))

    def ahead_y(t, part, z, v):
        halo = pltpu.roll(yd_r[t], W - 1 - part * NZ - z, 1)
        return jnp.where(lane == W - 1, halo, pltpu.roll(v, W - 1, 1))

    def step(t, sr, si, dr, di):
        def body(z, carry, az_r, az_i):
            bz_r, bz_i = carry
            r, i = sr[z], si[z]
            lap_r = -6.0 * r + bz_r
            lap_i = -6.0 * i + bz_i
            c, s = cs[0, z], cs[1, z]
            lap_r = lap_r + c * az_r - s * az_i
            lap_i = lap_i + c * az_i + s * az_r
            nz_r, nz_i = c * r + s * i, c * i - s * r
            c, s = cs[2, z], cs[3, z]
            a_r, a_i = ahead_x(t, 0, z, r), ahead_x(t, 1, z, i)
            lap_r = lap_r + c * a_r - s * a_i
            lap_i = lap_i + c * a_i + s * a_r
            q_r, q_i = c * r + s * i, c * i - s * r
            lap_r = lap_r + jnp.where(row == 0, xu_r[t, 0, pl.ds(z, 1), :], pltpu.roll(q_r, 1, 0))
            lap_i = lap_i + jnp.where(row == 0, xu_r[t, 1, pl.ds(z, 1), :], pltpu.roll(q_i, 1, 0))
            c, s = cs[4, z], cs[5, z]
            a_r, a_i = ahead_y(t, 0, z, r), ahead_y(t, 1, z, i)
            lap_r = lap_r + c * a_r - s * a_i
            lap_i = lap_i + c * a_i + s * a_r
            q_r, q_i = c * r + s * i, c * i - s * r
            h_r = pltpu.roll(yu_r[t], (W - z) % W, 1)
            h_i = pltpu.roll(yu_r[t], W - NZ - z, 1)
            lap_r = lap_r + jnp.where(lane == 0, h_r, pltpu.roll(q_r, 1, 1))
            lap_i = lap_i + jnp.where(lane == 0, h_i, pltpu.roll(q_i, 1, 1))
            g = eps[z] - (r * r + i * i)
            dr[z] = r + DT * (g * r + lap_r)
            di[z] = i + DT * (g * i + lap_i)
            return nz_r, nz_i

        def run(start, stop, carry):
            inner = min(stop, NZ - 1)
            carry = lax.fori_loop(
                start, inner, lambda z, c: body(z, c, sr[z + 1], si[z + 1]), carry)
            if stop == NZ:
                carry = body(NZ - 1, carry, zd_r[t, 0], zd_r[t, 1])
            return carry

        return run

    s_r, s_i = st.at[0], st.at[1]
    arrive(rounds[0])
    step(0, o_r, o_i, s_r, s_i)(0, NZ, (zu_r[0, 0], zu_r[0, 1]))
    edges(1, s_r, s_i)
    launch(rounds[1])
    mine = pl.ds(pl.multiple_of(gy * R, R), R)

    def slab_copy(b, k):
        to = lax.rem(gy + k, G)
        rows = pl.ds(pl.multiple_of(to * R, R), R)
        return pltpu.make_async_remote_copy(
            src_ref=jj.at[b, :, :, rows, :], dst_ref=rj.at[b, k], send_sem=jsnd.at[b * G + k],
            recv_sem=jrcv.at[b * G + k], device_id=at_device(gy=to), device_id_type=MESH)

    def row_copy(b, k):
        to = lax.rem(gy + k, G)
        return pltpu.make_async_remote_copy(
            src_ref=e_s.at[b, to], dst_ref=e_r.at[b, k], send_sem=esnd.at[b * (G + 1) + k],
            recv_sem=ercv.at[b * G + k], device_id=at_device(gy=to), device_id_type=MESH)

    def last_row_copy(b, k):
        return pltpu.make_async_remote_copy(
            src_ref=e_s.at[b, G - 1], dst_ref=e_r.at[b, k], send_sem=esnd.at[b * (G + 1) + G],
            recv_sem=ercv.at[b * G + k],
            device_id=at_device(gx=jnp.maximum(gx - 1, 0), gy=G - 1), device_id_type=MESH)

    @pl.when((gy == G - 1) & (gx == GX - 1))
    def _():
        e_r[...] = jnp.zeros_like(e_r)

    def faces(b):
        zs = range(b * ZC, (b + 1) * ZC)
        first_r = pack_cols([lambda z=z: fr[z] for z in zs], 0, NX)
        first_i = pack_cols([lambda z=z: fi[z] for z in zs], 0, NX)
        fy_s[b] = jnp.where(lane < ZC, first_r, pltpu.roll(first_i, ZC, 1))
        for j, z in enumerate(zs):
            fx_s[b, j:j + 1, :] = fr[z, 0:1, :]
            fx_s[b, ZC + j:ZC + j + 1, :] = fi[z, 0:1, :]

    def currents(b):
        def near_x(part, j, v):
            halo = fx_r[b, pl.ds(part * ZC + j, 1), :]
            return jnp.where(row == NX - 1, halo, pltpu.roll(v, NX - 1, 0))

        def near_y(part, j, v):
            halo = pltpu.roll(fy_r[b], W - 1 - part * ZC - j, 1)
            return jnp.where(lane == W - 1, halo, pltpu.roll(v, W - 1, 1))

        def body(j, _):
            z = b * ZC + j
            r, i = fr[z], fi[z]
            c, s = cs[2, z], cs[3, z]
            a_r, a_i = near_x(0, j, r), near_x(1, j, i)
            jj[b, 0, j] = r * (c * a_i + s * a_r) - i * (c * a_r - s * a_i)
            c, s = cs[4, z], cs[5, z]
            a_r, a_i = near_y(0, j, r), near_y(1, j, i)
            j_y = r * (c * a_i + s * a_r) - i * (c * a_r - s * a_i)
            jj[b, 1, j] = j_y
            for d in range(G):
                at = (R * (d + 1)) % NX
                e_s[b, d, pl.ds(j, 1), :] = j_y[at:at + 1, :]
            return 0

        lax.fori_loop(0, ZC, body, 0)

    def send(b):
        for k in range(1, G):
            pl.when(lax.rem(gy + k, G) != G - 1)(row_copy(b, k).start)
        pl.when(gx > 0)(last_row_copy(b, G - 1 - gy).start)
        for k in range(1, G):
            slab_copy(b, k).start()
        rj[b, 0] = jj[b, :, :, mine, :]

        @pl.when(gy < G - 1)
        def _():
            e_r[b, 0] = e_s[b, gy]

    def receive(b):
        for k in range(1, G):
            slab_copy(b, k).wait_recv()

        @pl.when(gy < G - 1)
        def _():
            for k in range(1, G):
                row_copy(b, k).wait_recv()

        @pl.when((gy == G - 1) & (gx < GX - 1))
        def _():
            for k in range(G):
                last_row_copy(b, k).wait_recv()

    rows_n = ZC * R
    lane_s = iota((rows_n, W), 1)
    row_s = iota((ZC, R, W), 1)
    slot = [lax.rem(gy - s + G, G) for s in range(G)]

    def slab(b):
        zs = slice(b * ZC, (b + 1) * ZC)
        jx = [rj[b, slot[s], 0].reshape(rows_n, W) for s in range(G)]
        total = jnp.zeros((rows_n, 1), jnp.float32)
        for s in range(G):
            v = jx[s]
            d = 1
            while d < W:
                v = v + jnp.where(lane_s >= d, pltpu.roll(v, d, 1), 0.0)
                d *= 2
            v = v + total
            total = v[:, W - 1:W]
            flux[zs, :, s * W:(s + 1) * W] = v.reshape(ZC, R, W)
            j_y = rj[b, slot[s], 1]
            extra = e_r[b, slot[s]].reshape(ZC, 1, W)
            j_y_next = jnp.where(row_s == R - 1, extra, pltpu.roll(j_y, R - 1, 1))
            after = jx[s + 1][:, 0:1] if s < G - 1 else jnp.zeros((rows_n, 1), jnp.float32)
            j_x_next = jnp.where(lane_s == W - 1, after, pltpu.roll(jx[s], W - 1, 1))
            circ[zs, :, s * W:(s + 1) * W] = (
                (jx[s] - j_x_next).reshape(ZC, R, W) + j_y_next - j_y)

    def store(b, n, src, dst):
        zs = pl.ds(b * ZC, ZC)
        return pltpu.make_async_copy(src.at[zs], dst.at[zs], outsem.at[4 * b + n])

    outs = [[store(b, n, src, dst) for n, (src, dst) in enumerate(
        ((fr, g0), (fi, g1), (circ, g2), (flux, g3)))] for b in range(NB)]

    arrive(rounds[1])
    second = step(1, s_r, s_i, fr, fi)
    carry = (zu_r[1, 0], zu_r[1, 1])
    for b in range(NB + 1):
        if b < NB:
            carry = second(b * ZC, (b + 1) * ZC, carry)
            faces(b)
            launch(final[b])
            outs[b][0].start()
            outs[b][1].start()
        if b > 0:
            arrive(final[b - 1])
            currents(b - 1)
            send(b - 1)
    for b in range(NB):
        receive(b)
        slab(b)
        outs[b][2].start()
        outs[b][3].start()

    for msgs in rounds + final:
        for copy, scond, _, _ in msgs:
            pl.when(scond)(copy.wait_send)
    for b in range(NB):
        for copy in outs[b]:
            copy.wait()
        for k in range(1, G):
            slab_copy(b, k).wait_send()
            pl.when(lax.rem(gy + k, G) != G - 1)(row_copy(b, k).wait_send)
        pl.when(gx > 0)(last_row_copy(b, 0).wait_send)


def place(*refs):
    n = (len(refs) - 2) // 3
    src, dst, mid, insem, outsem = refs[:n], refs[n:2 * n], refs[2 * n:3 * n], refs[-2], refs[-1]
    loads = [pltpu.make_async_copy(src[k], mid[k], insem.at[k]) for k in range(n)]
    saves = [pltpu.make_async_copy(mid[k], dst[k], outsem.at[k]) for k in range(n)]
    for load in loads:
        load.start()
    for load, save in zip(loads, saves):
        load.wait()
        save.start()
    for save in saves:
        save.wait()


def solution(mesh):
    GX, GY, GZ = (mesh.shape[a] for a in ("gx", "gy", "gz"))

    def shards(o_r, o_i, p_z, p_x, p_y, mat, lev):
        NZ, NX, NY = o_r.shape
        assert NY == W and 2 * NZ <= W and NX % (8 * GY) == 0 and NZ % ZC == 0
        R = NX // GY
        f32 = jnp.float32
        T = STEPS
        NB = NZ // ZC
        vm = lambda *shape: pltpu.VMEM(shape, f32)
        hspec = pl.BlockSpec(memory_space=pl.ANY)
        sspec = pl.BlockSpec(memory_space=pltpu.SMEM)
        dma = pltpu.SemaphoreType.DMA
        layers = lambda: [vm(T, 2, NX, W), vm(T, 2, NX, W), vm(T, 2, NZ, W), vm(T, 2, NZ, W),
                          vm(T, NX, W), vm(T, NX, W)]
        shapes = ([jax.ShapeDtypeStruct((NZ, NX, W), f32)] * 2
                  + [jax.ShapeDtypeStruct((NZ, R, GY * W), f32)] * 2)
        bufs = [vm(*shape.shape) for shape in shapes]
        results = pl.pallas_call(
            functools.partial(kernel, (NZ, NX, R, GX, GY, GZ)),
            out_shape=shapes,
            in_specs=[hspec] * 6 + [sspec],
            out_specs=[hspec] * 4,
            scratch_shapes=bufs + [vm(NZ, NX, W)] * 5 + [pltpu.VMEM((NZ, NX, W), jnp.int32)]
            + [vm(6, NZ, NX, W), vm(NZ, NX, W), vm(2, NZ, NX, W)]
            + layers() + layers()
            + [vm(2, NZ, W), vm(2, NX, W), vm(2, NX, W),
               vm(NB, 2, ZC, NX, W), vm(NB, GY, 2, ZC, R, W), vm(NB, GY, ZC, W), vm(NB, GY, ZC, W),
               vm(NB, 2 * ZC, W), vm(NB, 2 * ZC, W), vm(NB, NX, W), vm(NB, NX, W),
               dma((6,)), dma((4 * NB,)), dma((6 * T,)), dma((6 * T,)), dma((NB * GY,)), dma((NB * GY,)),
               dma((NB * (GY + 1),)), dma((NB * GY,)), dma((2 * NB,)), dma((2 * NB,))],
            compiler_params=pltpu.CompilerParams(
                collective_id=0, has_side_effects=True, vmem_limit_bytes=60 * 1024 * 1024),
        )(o_r, o_i, p_z, p_x, p_y, mat, lev)
        return pl.pallas_call(
            place, out_shape=shapes, in_specs=[hspec] * 4, out_specs=[hspec] * 4,
            scratch_shapes=bufs + [dma((4,)), dma((4,))],
            compiler_params=pltpu.CompilerParams(vmem_limit_bytes=60 * 1024 * 1024),
        )(*results)

    block = P("gz", "gx", "gy")
    line = P("gz", ("gx", "gy"), None)
    return jax.shard_map(shards, mesh=mesh, in_specs=(block,) * 6 + (P(),),
                         out_specs=(block, block, line, line), check_vma=False)
```
